32 devices in a mesh: mp: 2 (over y), row: 4 (over x, core), col: 4 (over z).
Axes of the slice: x: 2, y: 2, z: 4, core: 2. Of those that a mesh axis runs over, the one named last changes fastest.
Arguments:
- text_embeds: bfloat16 [160, 8192], P('row', 'col'), may hold values from -6 to 6
- image_embeds: bfloat16 [64, 8192], P(('mp', 'row'), 'col'), may hold values from -6 to 6
- offsets: int32 [4], replicated, may hold values from 0 to 16, as said below
- lengths: int32 [4], replicated, may hold values from 32 to 40
- loss_mask: int32 [160], P('row'), may hold values 0 or 1
- norm_gain: bfloat16 [2, 8192], P('mp', 'col'), may hold values from 0.5 to 1.5
- unembed_rows: bfloat16 [2, 160, 8192], P('mp', 'row', 'col'), may hold values from -0.0625 to 0.0625
- gate_up: bfloat16 [2, 8192, 2, 29568], P('mp', 'col', None, 'row'), may hold values from -0.0625 to 0.0625
- down_proj: bfloat16 [2, 29568, 8192], P('mp', 'row', 'col'), may hold values from -0.03125 to 0.03125
Outputs:
- dpo_loss: float32 [], replicated
- input_grad: float32 [160, 8192], P(('mp', 'row'), 'col')
The draws below stay inside these ranges and needn't reach their ends.
Inputs may be any that keep to these rules, and one draw needn't show every extreme that they name: Each sequence's image tokens end at least 8 positions before its end: offsets[s] + 24 <= 40. Tokens at or after lengths[s] are padding and never scored.
All inputs are finite; a program needn't handle non-finite values. No bound on the sum of `loss_mask` on one device may be relied on, other than what follows from the above.
Results may differ from the reference program's by a relative error of at most 0.035.
Values may be sent and summed in bfloat16 or wider, within the bound.
No kernel may reach another device: no remote copies, remote signals or barrier semaphores. Data moves between devices by JAX's collectives and lax.ppermute only.
A program may use at most 192 MiB of HBM per device.

```python
import jax
import jax.numpy as jnp
from jax import lax

D = 8192
FF = 29568
SEQ = 40
IMG = 16
NSEQ = 4
TOKENS = 160
N_COL = 4


align_weight = 0.7


noise_weight = 0.71


clip_value = 0.0625


def embed_fields(key):
    text_key = jax.random.fold_in(key, 101)
    image_key = jax.random.fold_in(key, 202)
    text_field = jnp.clip(jax.random.normal(text_key, (TOKENS, D), jnp.float32), -6.0, 6.0)
    image_field = jnp.clip(jax.random.normal(image_key, (NSEQ * IMG, D), jnp.float32), -6.0, 6.0)
    return (text_field, image_field)


def offset_values(key):
    drawn_offsets = jax.random.randint(jax.random.fold_in(key, 303), (NSEQ,), 0, SEQ - IMG - 7, dtype=jnp.int32)
    shuffled = jax.random.permutation(jax.random.fold_in(key, 304), NSEQ)
    drawn_offsets = drawn_offsets.at[shuffled[0]].set(SEQ - IMG - 8)
    drawn_offsets = drawn_offsets.at[shuffled[1]].set(0)
    return drawn_offsets.astype(jnp.int32)


def draw_text_embeds(key, part):
    text_field, image_field = embed_fields(key)
    return text_field.astype(jnp.bfloat16)


def draw_image_embeds(key, part):
    text_field, image_field = embed_fields(key)
    return image_field.astype(jnp.bfloat16)


def draw_offsets(key, part):
    return offset_values(key)


def draw_unembed_rows(key, part):
    text_field, image_field = embed_fields(key)
    first_positions = offset_values(key)
    global_pos = jnp.arange(TOKENS, dtype=jnp.int32)
    position = global_pos % SEQ
    seq_id = global_pos // SEQ
    first_img = first_positions[seq_id]
    inside = (position >= first_img) & (position < first_img + IMG)
    source = jnp.clip(seq_id * IMG + position - first_img, 0, NSEQ * IMG - 1).astype(jnp.int32)
    placed = jnp.where(inside[:, None], jnp.take(image_field, source, axis=0), text_field)
    token_signs = (jax.random.randint(jax.random.fold_in(key, 405), (TOKENS,), 0, 2, dtype=jnp.int32) * 2 - 1).astype(jnp.float32)
    noise_key = jax.random.fold_in(key, 406)
    noise_field = jax.random.normal(noise_key, (2, TOKENS, D), jnp.float32)
    scale_factor = D ** (-0.5)
    aligned = align_weight * token_signs[:, None] * placed
    rows_value = scale_factor * (aligned[None, :, :] + noise_weight * noise_field)
    return jnp.clip(rows_value, -clip_value, clip_value).astype(jnp.bfloat16)


def plant(drawn, key, low, largest):
    index_at = [jax.random.randint(jax.random.fold_in(key, axis), (), 0, length) for axis, length in enumerate(drawn.shape)]
    longest = drawn.shape.index(max(drawn.shape))
    next_to = index_at[:longest] + [(index_at[longest] + 1) % drawn.shape[longest]] + index_at[longest + 1:]
    return drawn.at[tuple(index_at)].set(low).at[tuple(next_to)].set(largest)


def levels(rng, extent, shards, least, top_value):
    def one(dim, parts):
        draws = jax.random.uniform(jax.random.fold_in(jax.random.fold_in(rng, 6), dim), (parts,), jnp.float32, least / len(shards), top_value / len(shards))
        return jnp.repeat(jnp.exp(draws), extent[dim] // parts).reshape((-1,) + (1,) * (len(extent) - dim - 1))

    factor_of = one(*shards[0])
    for cut in shards[1:]:
        factor_of = factor_of * one(*cut)
    return factor_of


def scatter_about(stream_key, dims, spread, most, shards=(), kind=jnp.bfloat16):
    factor_of = levels(stream_key, dims, shards, -0.22, 0.18) if shards else 1.0
    array = jax.random.normal(stream_key, dims, jnp.float32) * spread * factor_of
    return jnp.minimum(jnp.maximum(array, -most), most).astype(kind)


def setup_inputs(seed: int = 0) -> dict:
    seeds = jax.random.split(jax.random.key(seed), 10)
    return {
        "text_embeds": draw_text_embeds(jax.random.fold_in(seeds[9], 71), 0),
        "image_embeds": draw_image_embeds(jax.random.fold_in(seeds[9], 71), 0),
        "offsets": draw_offsets(jax.random.fold_in(seeds[9], 71), 0),
        "lengths": plant(jax.random.randint(seeds[3], (NSEQ,), SEQ - 8, SEQ + 1), jax.random.fold_in(seeds[3], 1), SEQ - 8, SEQ).astype(jnp.int32),
        "loss_mask": plant((jax.random.randint(seeds[4], (TOKENS,), 0, 4) < 3).astype(jnp.int32), jax.random.fold_in(seeds[4], 1), 0, 1),
        "norm_gain": jnp.clip(1.0 + 0.1 * jax.random.normal(seeds[5], (2, D), jnp.float32), 0.5, 1.5).astype(jnp.bfloat16),
        "unembed_rows": draw_unembed_rows(jax.random.fold_in(seeds[9], 71), 0),
        "gate_up": scatter_about(seeds[7], (2, D, 2, FF), D ** -0.5, 0.0625, ((0, 2), (1, 4), (3, 4))),
        "down_proj": scatter_about(seeds[8], (2, FF, D), FF ** -0.5, 0.03125, ((0, 2), (1, 4), (2, 4))),
    }


dpo_beta = 0.1
norm_eps = 1e-06

def place_images(text_rows, images, offsets):
    tokens = text_rows.shape[0]
    global_pos = jnp.arange(tokens, dtype=jnp.int32)
    position = global_pos % SEQ
    seq_id = global_pos // SEQ
    first_img = offsets[seq_id]
    inside = (position >= first_img) & (position < first_img + IMG)
    source = jnp.clip(seq_id * IMG + position - first_img, 0, images.shape[0] - 1).astype(jnp.int32)
    return jnp.where(inside[:, None], jnp.take(images, source, axis=0), text_rows)

def dpo_terms(totals):
    policy = totals[0]
    frozen = totals[1]
    margin = policy[0::2] - frozen[0::2] - (policy[1::2] - frozen[1::2])
    loss_value = jnp.mean(jax.nn.softplus(-dpo_beta * margin))
    dmargin = -dpo_beta * jax.nn.sigmoid(-dpo_beta * margin) / margin.shape[0]
    return (loss_value, dmargin)

def gate_up_sums(inputs, weight):
    block_width = inputs.shape[1] // N_COL

    def add_block(running, block_id):
        columns = lax.dynamic_slice_in_dim(inputs, block_id * block_width, block_width, 1)
        weight_rows = lax.dynamic_slice_in_dim(weight, block_id * block_width, block_width, 0)
        partial_value = jnp.dot(columns, weight_rows, preferred_element_type=jnp.float32).astype(jnp.bfloat16)
        partial_value = lax.optimization_barrier(partial_value)
        return (running + partial_value.astype(jnp.float32), None)
    start_value = jnp.zeros((inputs.shape[0], weight.shape[1]), jnp.float32)
    running, unused = lax.scan(add_block, start_value, jnp.arange(N_COL, dtype=jnp.int32))
    return running

def reference(text_embeds, image_embeds, offsets, lengths, loss_mask, norm_gain, unembed_rows, gate_up, down_proj):
    inputs = place_images(text_embeds, image_embeds, offsets)
    tokens = inputs.shape[0]
    global_pos = jnp.arange(tokens, dtype=jnp.int32)
    position = global_pos % SEQ
    seq_id = global_pos // SEQ
    scored = ((position < lengths[seq_id]) & (loss_mask == 1)).astype(jnp.float32)
    saved = []
    seq_list = []
    for model_id in range(2):
        weight = gate_up[model_id].reshape(D, 2 * FF)
        pre_sums = gate_up_sums(inputs, weight)
        gate_part = pre_sums[:, :FF]
        up_part = pre_sums[:, FF:]
        hidden = (jax.nn.silu(gate_part) * up_part).astype(jnp.bfloat16)
        residual = inputs.astype(jnp.float32) + jnp.dot(hidden, down_proj[model_id], preferred_element_type=jnp.float32)
        coeff = norm_gain[model_id].astype(jnp.float32)[None, :] * unembed_rows[model_id].astype(jnp.float32)
        squares = lax.optimization_barrier(jnp.sum(residual * residual, axis=1))
        cross_term = lax.optimization_barrier(jnp.sum(residual * coeff, axis=1))
        inv_rms = lax.rsqrt(squares / D + norm_eps)
        tok_score = cross_term * inv_rms
        seq_list.append(lax.optimization_barrier(jnp.sum((scored * tok_score).reshape(-1, SEQ), axis=1)))
        saved.append((weight, gate_part, up_part, residual, coeff, cross_term, inv_rms))
    totals = jnp.stack(seq_list)
    loss_value, dmargin = dpo_terms(totals)
    weight, gate_part, up_part, residual, coeff, cross_term, inv_rms = saved[0]
    seq_grad = jnp.stack([dmargin, -dmargin], axis=1).reshape(-1)
    dscore = scored * jnp.repeat(seq_grad, SEQ)
    dresid = dscore[:, None] * (inv_rms[:, None] * coeff - (cross_term * inv_rms ** 3 / D)[:, None] * residual)
    dy_rows = dresid.astype(jnp.bfloat16)
    dhidden = jnp.dot(dy_rows, down_proj[0].T, preferred_element_type=jnp.float32)
    sigmoid_gate = jax.nn.sigmoid(gate_part)
    gate_grad = dhidden * up_part * sigmoid_gate * (1.0 + gate_part * (1.0 - sigmoid_gate))
    up_grad = dhidden * gate_part * sigmoid_gate
    pre_grad = jnp.concatenate([gate_grad, up_grad], axis=1).astype(jnp.bfloat16)
    input_grad = dresid + jnp.dot(pre_grad, weight.T, preferred_element_type=jnp.float32)
    return (loss_value, input_grad)
```

```python
import functools

import jax
import jax.numpy as jnp
from jax import lax
from jax.experimental import pallas as pl
from jax.experimental.pallas import tpu as pltpu
from jax.sharding import PartitionSpec as P

D = 8192
SEQ = 40
IMG = 16


dpo_beta = 0.1
norm_eps = 1e-06

CHUNKS = 4
VMEM_LIMIT = 48 * 1024 * 1024
BF16 = jnp.bfloat16
F32 = jnp.float32


def place_images(text_rows, images, offsets):
    tokens = text_rows.shape[0]
    global_pos = jnp.arange(tokens, dtype=jnp.int32)
    position = global_pos % SEQ
    seq_id = global_pos // SEQ
    first_img = offsets[seq_id]
    inside = (position >= first_img) & (position < first_img + IMG)
    source = jnp.clip(seq_id * IMG + position - first_img, 0, images.shape[0] - 1)
    return jnp.where(inside[:, None], jnp.take(images, source, axis=0), text_rows)


def dpo_terms(totals):
    policy = totals[0]
    frozen = totals[1]
    margin = policy[0::2] - frozen[0::2] - (policy[1::2] - frozen[1::2])
    loss_value = jnp.mean(jax.nn.softplus(-dpo_beta * margin))
    dmargin = -dpo_beta * jax.nn.sigmoid(-dpo_beta * margin) / margin.shape[0]
    return (loss_value, dmargin)


def dot_transposed(left, right):
    return lax.dot_general(
        left, right, (((1,), (1,)), ((), ())), preferred_element_type=jnp.float32
    )


def general(
    text_embeds,
    image_embeds,
    offsets,
    lengths,
    loss_mask,
    norm_gain,
    unembed_rows,
    gate_up,
    down_proj,
):
    text_full = lax.all_gather(text_embeds, "row", axis=0, tiled=True)
    images = lax.all_gather(image_embeds, ("mp", "row"), axis=0, tiled=True)
    inputs = place_images(text_full, images, offsets)
    tokens = inputs.shape[0]
    local_rows = tokens // lax.axis_size("row")
    hidden_width = gate_up.shape[3]
    weight = gate_up[0].reshape(gate_up.shape[1], 2 * hidden_width)
    down_block = down_proj[0]
    row_start = lax.axis_index("row") * local_rows
    pre_sums = lax.psum_scatter(
        jnp.dot(inputs, weight, preferred_element_type=jnp.float32).astype(jnp.bfloat16),
        "col",
        scatter_dimension=0,
        tiled=True,
    ).astype(jnp.float32)
    gate_part = pre_sums[:, :hidden_width]
    up_part = pre_sums[:, hidden_width:]
    hidden = (jax.nn.silu(gate_part) * up_part).astype(jnp.bfloat16)
    out_partial = jnp.dot(
        lax.all_gather(hidden, "col", axis=0, tiled=True),
        down_block,
        preferred_element_type=jnp.float32,
    )
    block_out = lax.psum_scatter(
        out_partial.astype(jnp.bfloat16), "row", scatter_dimension=0, tiled=True
    ).astype(jnp.float32)
    own_rows = lax.dynamic_slice_in_dim(inputs, row_start, local_rows, 0)
    residual = own_rows.astype(jnp.float32) + block_out
    coeff = norm_gain[0].astype(jnp.float32)[None, :] * unembed_rows[0].astype(jnp.float32)
    squares, cross_term = lax.psum(
        (jnp.sum(residual * residual, axis=1), jnp.sum(residual * coeff, axis=1)), "col"
    )
    inv_rms = lax.rsqrt(squares / D + norm_eps)
    tok_score = cross_term * inv_rms
    global_pos = row_start + jnp.arange(local_rows, dtype=jnp.int32)
    position = global_pos % SEQ
    seq_id = global_pos // SEQ
    scored = ((position < lengths[seq_id]) & (loss_mask == 1)).astype(jnp.float32)
    seq_count = offsets.shape[0]
    onehot = (seq_id[:, None] == jnp.arange(seq_count, dtype=jnp.int32)[None, :]).astype(
        jnp.float32
    )
    seq_part = jnp.dot(scored * tok_score, onehot, precision=lax.Precision.HIGHEST)
    model_id = lax.axis_index("mp")
    score_slots = (jnp.arange(2, dtype=jnp.int32) == model_id).astype(jnp.float32)[
        :, None
    ] * seq_part[None, :]
    totals = lax.psum(score_slots, ("mp", "row"))
    loss_value, dmargin = dpo_terms(totals)
    policy_flag = (model_id == 0).astype(jnp.float32)
    seq_grad = policy_flag * jnp.stack([dmargin, -dmargin], axis=1).reshape(seq_count)
    dscore = scored * jnp.dot(onehot, seq_grad, precision=lax.Precision.HIGHEST)
    dresid = dscore[:, None] * (
        inv_rms[:, None] * coeff - (cross_term * inv_rms**3 / D)[:, None] * residual
    )
    dy_full = lax.all_gather(dresid.astype(jnp.bfloat16), "row", axis=0, tiled=True)
    dhidden = lax.psum_scatter(
        dot_transposed(dy_full, down_block).astype(jnp.bfloat16),
        "col",
        scatter_dimension=0,
        tiled=True,
    ).astype(jnp.float32)
    sigmoid_gate = jax.nn.sigmoid(gate_part)
    gate_grad = dhidden * up_part * sigmoid_gate * (1.0 + gate_part * (1.0 - sigmoid_gate))
    up_grad = dhidden * gate_part * sigmoid_gate
    pre_grad = jnp.concatenate([gate_grad, up_grad], axis=1).astype(jnp.bfloat16)
    input_partial = dot_transposed(lax.all_gather(pre_grad, "col", axis=0, tiled=True), weight)
    placed = lax.dynamic_update_slice_in_dim(jnp.zeros_like(input_partial), dresid, row_start, 0)
    input_grad = lax.psum_scatter(
        (input_partial + placed).astype(jnp.bfloat16),
        ("mp", "row"),
        scatter_dimension=0,
        tiled=True,
    ).astype(jnp.float32)
    return (loss_value, input_grad)


def swap(value, axis, mask, size):
    return lax.ppermute(value, axis, [(i, i ^ mask) for i in range(size)])


def inward(value):
    return lax.ppermute(value, "col", [(0, 1), (3, 2)])


def across(value):
    return lax.ppermute(value, "col", [(1, 2), (2, 1)])


def outward(value):
    return lax.ppermute(value, "col", [(1, 0), (2, 3)])


def reduce_to_ends(near, far):
    passed = far + inward(far)
    gathered = near + across(passed)
    return gathered.astype(F32) + outward(gathered).astype(F32)


def spread_from_ends(value, is_end):
    near = jnp.where(is_end, value, inward(value))
    crossed = across(near)
    return near, crossed, outward(crossed)


def pieces_of(extent, step):
    return [(a, min(a + step, extent)) for a in range(0, extent, step)]


def rows_kernel(start, pieces, x_ref, w_ref, near_ref, far_ref, held, sems):
    half = x_ref.shape[0] // 2
    copies = []
    for g in range(w_ref.shape[0]):
        for i, (a, b) in enumerate(pieces):
            copy = pltpu.make_async_copy(
                w_ref.at[g, pl.ds(start + a, b - a), :],
                held.at[g, pl.ds(a, b - a), :],
                sems.at[g, i],
            )
            copy.start()
            copies.append((g, a, b, copy))
    for g, a, b, copy in copies:
        copy.wait()
        product = dot_transposed(x_ref[...], held[g, a:b, :]).astype(near_ref.dtype)
        near_ref[g * half : (g + 1) * half, a:b] = product[:half]
        far_ref[g * half : (g + 1) * half, a:b] = product[half:]


def times_rows(x, w, start, width):
    tokens, depth = x.shape
    count = w.shape[0]
    pieces = pieces_of(width, 384)
    shape = jax.ShapeDtypeStruct((count * tokens // 2, width), BF16)
    return pl.pallas_call(
        functools.partial(rows_kernel, start, pieces),
        out_shape=(shape, shape),
        in_specs=[pl.BlockSpec(memory_space=pltpu.VMEM), pl.BlockSpec(memory_space=pl.ANY)],
        out_specs=(pl.BlockSpec(memory_space=pltpu.VMEM),) * 2,
        scratch_shapes=[
            pltpu.VMEM((count, width, depth), w.dtype),
            pltpu.SemaphoreType.DMA((count, len(pieces))),
        ],
        compiler_params=pltpu.CompilerParams(vmem_limit_bytes=VMEM_LIMIT),
        cost_estimate=pl.CostEstimate(
            flops=2 * tokens * depth * width * count,
            bytes_accessed=2 * depth * width * count,
            transcendentals=0,
        ),
    )(x, w)


def columns_kernel(start, pieces, first, *refs):
    if first:
        near_ref, far_a_ref, far_b_ref, w_ref, out_ref, held, left, sems = refs
    else:
        acc_ref, near_ref, far_a_ref, far_b_ref, w_ref, out_ref, held, left, sems = refs
    count, width = held.shape[0], held.shape[1]
    half = near_ref.shape[0] // count
    copies = []
    for i, (a, b) in enumerate(pieces):
        for g in range(count):
            copy = pltpu.make_async_copy(
                w_ref.at[g, pl.ds(start, width), pl.ds(a, b - a)],
                held.at[g, :, pl.ds(a, b - a)],
                sems.at[g, i],
            )
            copy.start()
            copies.append(copy)
    for g in range(count):
        left[g, :half] = near_ref[g * half : (g + 1) * half]
        left[g, half:] = (
            far_a_ref[g * half : (g + 1) * half] + far_b_ref[g * half : (g + 1) * half]
        )
    for i, (a, b) in enumerate(pieces):
        total = None if first else acc_ref[:, a:b]
        for g in range(count):
            copies[i * count + g].wait()
            product = jnp.dot(left[g], held[g, :, a:b], preferred_element_type=F32)
            total = product if total is None else total + product
        out_ref[:, a:b] = total


def times_columns(acc, near, far_a, far_b, w, start):
    count, _, depth = w.shape
    width = near.shape[1]
    tokens = 2 * near.shape[0] // count
    pieces = pieces_of(depth, 512)
    first = acc is None
    given = (near, far_a, far_b, w) if first else (acc, near, far_a, far_b, w)
    vmem = pl.BlockSpec(memory_space=pltpu.VMEM)
    return pl.pallas_call(
        functools.partial(columns_kernel, start, pieces, first),
        out_shape=jax.ShapeDtypeStruct((tokens, depth), F32),
        in_specs=[vmem] * (len(given) - 1) + [pl.BlockSpec(memory_space=pl.ANY)],
        out_specs=vmem,
        scratch_shapes=[
            pltpu.VMEM((count, width, depth), w.dtype),
            pltpu.VMEM((count, tokens, width), BF16),
            pltpu.SemaphoreType.DMA((count, len(pieces))),
        ],
        compiler_params=pltpu.CompilerParams(vmem_limit_bytes=VMEM_LIMIT),
        cost_estimate=pl.CostEstimate(
            flops=2 * tokens * depth * width * count,
            bytes_accessed=2 * depth * width * count,
            transcendentals=0,
        ),
    )(*given)


def line_of_four(
    text_embeds,
    image_embeds,
    offsets,
    lengths,
    loss_mask,
    norm_gain,
    unembed_rows,
    gate_up,
    down_proj,
):
    rows = text_embeds.shape[0]
    img_rows = image_embeds.shape[0]
    tokens = 4 * rows
    half = tokens // 2
    eighth = tokens // 8
    seq_count = offsets.shape[0]
    model_id = lax.axis_index("mp")
    row_id = lax.axis_index("row")
    col_id = lax.axis_index("col")
    chip_bit = row_id // 2
    core_bit = row_id % 2
    is_end = (col_id == 0) | (col_id == 3)
    right = (col_id >= 2).astype(jnp.int32)

    def token_at(place):
        side = (place // half) ^ right
        within = place % half
        block = within // eighth
        return side * half + ((block % 2) * 2 + block // 2) * eighth + within % eighth

    own = jnp.concatenate([text_embeds, image_embeds], axis=0)
    over_x = swap(own, "row", 2, 4)
    over_y = swap(image_embeds, "mp", 1, 2)
    over_xy = swap(image_embeds, ("mp", "row"), 6, 8)
    mine = jnp.concatenate([own, over_x, over_y, over_xy], axis=0)
    both = jnp.concatenate([mine, swap(mine, "row", 1, 4)], axis=0)
    core_span = mine.shape[0]
    grid = (tokens, 2 * core_span)
    token = token_at(lax.broadcasted_iota(jnp.int32, grid, 0))
    position = token % SEQ
    seq = token // SEQ
    first = jnp.zeros(grid, jnp.int32)
    for k in range(seq_count):
        first = jnp.where(seq == k, offsets[k], first)
    inside = (position >= first) & (position < first + IMG)
    block = token // rows
    text_src = (
        ((block % 2) ^ core_bit) * core_span
        + ((block // 2) ^ chip_bit) * (rows + img_rows)
        + token % rows
    )
    image = seq * IMG + position - first
    holder = image // img_rows
    img_chip = ((holder // 2) % 2) ^ chip_bit
    img_src = (
        ((holder % 2) ^ core_bit) * core_span
        + jnp.where(
            (holder // 4) == model_id,
            img_chip * (rows + img_rows) + rows,
            2 * (rows + img_rows) + img_chip * img_rows,
        )
        + image % img_rows
    )
    source = jnp.where(inside, img_src, text_src)
    pick = (source == lax.broadcasted_iota(jnp.int32, grid, 1)).astype(BF16)
    inputs = jnp.dot(pick, both, preferred_element_type=F32).astype(BF16)

    width = gate_up.shape[3] // CHUNKS
    weight = jnp.transpose(gate_up[0], (1, 2, 0))
    features = weight.shape[2]
    saved = []
    out_partial = None
    for k in range(CHUNKS):
        near, far = times_rows(inputs, weight, k * width, width)
        sums = reduce_to_ends(near, far)
        gate, up = sums[:half], sums[half:]
        saved.append((gate, up))
        hidden = (jax.nn.silu(gate) * up).astype(BF16)
        spread = spread_from_ends(hidden, is_end)
        out_partial = times_columns(out_partial, *spread, down_proj, k * width)

    mask_lanes = jnp.pad((loss_mask == 1).astype(BF16)[:, None], ((0, 0), (0, 127)))
    target_own = jnp.concatenate([unembed_rows[0], mask_lanes], axis=1)
    target = jnp.concatenate([target_own, swap(target_own, "row", 2, 4)], axis=0)
    target = jnp.concatenate([target, swap(target, "row", 1, 4)], axis=0)
    grid = (tokens, tokens)
    token = token_at(lax.broadcasted_iota(jnp.int32, grid, 0))
    block = token // rows
    source = (
        ((block % 2) ^ core_bit) * (2 * rows) + ((block // 2) ^ chip_bit) * rows + token % rows
    )
    pick = (source == lax.broadcasted_iota(jnp.int32, grid, 1)).astype(BF16)
    target = jnp.dot(pick, target, preferred_element_type=F32)
    coeff = norm_gain[0].astype(F32)[None, :] * target[:, :features]
    token = token_at(lax.broadcasted_iota(jnp.int32, (tokens, 1), 0))
    position = token % SEQ
    seq = token // SEQ
    length = jnp.zeros((tokens, 1), jnp.int32)
    for k in range(seq_count):
        length = jnp.where(seq == k, lengths[k], length)
    scored = jnp.where(position < length, target[:, features : features + 1], 0.0)

    def halves(value):
        lower, upper = value[:half], value[half:]
        return (
            jnp.where(core_bit == 0, lower, upper),
            jnp.where(core_bit == 0, upper, lower),
        )

    keep, give = halves(out_partial)
    pair = keep + swap(give.astype(BF16), "row", 1, 4).astype(F32)
    pair16 = pair.astype(BF16)
    summed = (pair16.astype(F32) + swap(pair16, "row", 2, 4).astype(F32)).astype(BF16)
    other = swap(summed, "row", 1, 4)
    block_out = jnp.where(
        core_bit == 0,
        jnp.concatenate([summed, other], axis=0),
        jnp.concatenate([other, summed], axis=0),
    )
    residual = inputs.astype(F32) + block_out.astype(F32)

    parts = jnp.stack([jnp.sum(residual * residual, axis=1), jnp.sum(residual * coeff, axis=1)])
    turned = jnp.concatenate([parts[:, half:], parts[:, :half]], axis=1)
    parts = jnp.where(right == 1, turned, parts)
    parts = parts + swap(parts, "col", 1, 4)
    parts = parts + swap(parts, "col", 2, 4)
    frozen = swap(parts, "mp", 1, 2)
    turn_back = lambda v: jnp.where(
        right == 1, jnp.concatenate([v[:, half:], v[:, :half]], axis=1), v
    )
    parts = turn_back(parts)
    frozen = turn_back(frozen)

    def seq_scores(sums):
        score = sums[1] * lax.rsqrt(sums[0] / D + norm_eps)
        per_token = jnp.where(scored > 0.0, score[:, None], 0.0)
        lanes = lax.broadcasted_iota(jnp.int32, (tokens, seq_count), 1)
        return jnp.sum(jnp.where(seq == lanes, per_token, 0.0), axis=0)

    mine_scores = seq_scores(parts)
    other_scores = seq_scores(frozen)
    is_policy = model_id == 0
    totals = jnp.stack(
        [
            jnp.where(is_policy, mine_scores, other_scores),
            jnp.where(is_policy, other_scores, mine_scores),
        ]
    )
    loss_value, dmargin = dpo_terms(totals)
    inv_rms = lax.rsqrt(parts[0] / D + norm_eps)[:, None]
    cross = parts[1][:, None]
    dscore = jnp.zeros((tokens, 1), F32)
    for k in range(seq_count):
        value = dmargin[k // 2] if k % 2 == 0 else -dmargin[k // 2]
        dscore = jnp.where(seq == k, value, dscore)
    dscore = jnp.where(is_policy & (scored > 0.0), dscore, 0.0)
    dresid = dscore * (inv_rms * coeff - (cross * inv_rms**3 / D) * residual)
    dy = dresid.astype(BF16)

    grad_partial = jnp.where(core_bit + 2 * chip_bit == 0, dresid, 0.0)
    for k in range(CHUNKS):
        gate, up = saved[k]
        near, far = times_rows(dy, down_proj, k * width, width)
        dhidden = reduce_to_ends(near, far)
        sigmoid_gate = jax.nn.sigmoid(gate)
        gate_grad = dhidden * up * sigmoid_gate * (1.0 + gate * (1.0 - sigmoid_gate))
        up_grad = dhidden * gate * sigmoid_gate
        pre_grad = jnp.concatenate([gate_grad, up_grad], axis=0).astype(BF16)
        spread = spread_from_ends(pre_grad, is_end)
        grad_partial = times_columns(grad_partial, *spread, weight, k * width)

    folded = grad_partial.reshape(2, 2, 2 * eighth, features)
    keep = jnp.where(core_bit == 0, folded[:, 0], folded[:, 1])
    give = jnp.where(core_bit == 0, folded[:, 1], folded[:, 0])
    pair = keep + swap(give.astype(BF16), "row", 1, 4).astype(F32)
    folded = pair.reshape(2, 2, eighth, features)
    keep = jnp.where(chip_bit == 0, folded[:, 0], folded[:, 1])
    give = jnp.where(chip_bit == 0, folded[:, 1], folded[:, 0])
    total = keep + swap(give.astype(BF16), "row", 2, 4).astype(F32)
    first_half = jnp.where(right == 0, total[0], total[1])
    second_half = jnp.where(right == 0, total[1], total[0]).astype(BF16)
    sent = lax.ppermute(second_half, "mp", [(0, 1)])
    input_grad = jnp.where(is_policy, first_half, sent.astype(F32))
    return (loss_value, input_grad)


def solution(mesh):
    in_specs = (
        P("row", "col"),
        P(("mp", "row"), "col"),
        P(),
        P(),
        P("row"),
        P("mp", "col"),
        P("mp", "row", "col"),
        P("mp", "col", None, "row"),
        P("mp", "row", "col"),
    )
    out_specs = (P(), P(("mp", "row"), "col"))
    sizes = dict(mesh.shape)
    if not (sizes["mp"] == 2 and sizes["row"] == 4 and sizes["col"] == 4):
        return jax.shard_map(
            general, mesh=mesh, in_specs=in_specs, out_specs=out_specs, check_vma=False
        )

    return jax.shard_map(line_of_four, mesh=mesh, in_specs=in_specs, out_specs=out_specs, check_vma=False)
```

```python
import functools

import jax
import jax.numpy as jnp
from jax import lax
from jax.experimental import pallas as pl
from jax.experimental.pallas import tpu as pltpu
from jax.sharding import PartitionSpec as P

D = 8192
SEQ = 40
IMG = 16


dpo_beta = 0.1
norm_eps = 1e-06

FORWARD = (1, 1, 1, 1)
STEP = 256
WIDE = 512
VMEM_LIMIT = 48 * 1024 * 1024
BF16 = jnp.bfloat16
F32 = jnp.float32


def place_images(text_rows, images, offsets):
    tokens = text_rows.shape[0]
    global_pos = jnp.arange(tokens, dtype=jnp.int32)
    position = global_pos % SEQ
    seq_id = global_pos // SEQ
    first_img = offsets[seq_id]
    inside = (position >= first_img) & (position < first_img + IMG)
    source = jnp.clip(seq_id * IMG + position - first_img, 0, images.shape[0] - 1)
    return jnp.where(inside[:, None], jnp.take(images, source, axis=0), text_rows)


def dpo_terms(totals):
    policy = totals[0]
    frozen = totals[1]
    margin = policy[0::2] - frozen[0::2] - (policy[1::2] - frozen[1::2])
    loss_value = jnp.mean(jax.nn.softplus(-dpo_beta * margin))
    dmargin = -dpo_beta * jax.nn.sigmoid(-dpo_beta * margin) / margin.shape[0]
    return (loss_value, dmargin)


def dot_transposed(left, right):
    return lax.dot_general(
        left, right, (((1,), (1,)), ((), ())), preferred_element_type=jnp.float32
    )


def general(
    text_embeds,
    image_embeds,
    offsets,
    lengths,
    loss_mask,
    norm_gain,
    unembed_rows,
    gate_up,
    down_proj,
):
    text_full = lax.all_gather(text_embeds, "row", axis=0, tiled=True)
    images = lax.all_gather(image_embeds, ("mp", "row"), axis=0, tiled=True)
    inputs = place_images(text_full, images, offsets)
    tokens = inputs.shape[0]
    local_rows = tokens // lax.axis_size("row")
    hidden_width = gate_up.shape[3]
    weight = gate_up[0].reshape(gate_up.shape[1], 2 * hidden_width)
    down_block = down_proj[0]
    row_start = lax.axis_index("row") * local_rows
    pre_sums = lax.psum_scatter(
        jnp.dot(inputs, weight, preferred_element_type=jnp.float32).astype(jnp.bfloat16),
        "col",
        scatter_dimension=0,
        tiled=True,
    ).astype(jnp.float32)
    gate_part = pre_sums[:, :hidden_width]
    up_part = pre_sums[:, hidden_width:]
    hidden = (jax.nn.silu(gate_part) * up_part).astype(jnp.bfloat16)
    out_partial = jnp.dot(
        lax.all_gather(hidden, "col", axis=0, tiled=True),
        down_block,
        preferred_element_type=jnp.float32,
    )
    block_out = lax.psum_scatter(
        out_partial.astype(jnp.bfloat16), "row", scatter_dimension=0, tiled=True
    ).astype(jnp.float32)
    own_rows = lax.dynamic_slice_in_dim(inputs, row_start, local_rows, 0)
    residual = own_rows.astype(jnp.float32) + block_out
    coeff = norm_gain[0].astype(jnp.float32)[None, :] * unembed_rows[0].astype(jnp.float32)
    squares, cross_term = lax.psum(
        (jnp.sum(residual * residual, axis=1), jnp.sum(residual * coeff, axis=1)), "col"
    )
    inv_rms = lax.rsqrt(squares / D + norm_eps)
    tok_score = cross_term * inv_rms
    global_pos = row_start + jnp.arange(local_rows, dtype=jnp.int32)
    position = global_pos % SEQ
    seq_id = global_pos // SEQ
    scored = ((position < lengths[seq_id]) & (loss_mask == 1)).astype(jnp.float32)
    seq_count = offsets.shape[0]
    onehot = (seq_id[:, None] == jnp.arange(seq_count, dtype=jnp.int32)[None, :]).astype(
        jnp.float32
    )
    seq_part = jnp.dot(scored * tok_score, onehot, precision=lax.Precision.HIGHEST)
    model_id = lax.axis_index("mp")
    score_slots = (jnp.arange(2, dtype=jnp.int32) == model_id).astype(jnp.float32)[
        :, None
    ] * seq_part[None, :]
    totals = lax.psum(score_slots, ("mp", "row"))
    loss_value, dmargin = dpo_terms(totals)
    policy_flag = (model_id == 0).astype(jnp.float32)
    seq_grad = policy_flag * jnp.stack([dmargin, -dmargin], axis=1).reshape(seq_count)
    dscore = scored * jnp.dot(onehot, seq_grad, precision=lax.Precision.HIGHEST)
    dresid = dscore[:, None] * (
        inv_rms[:, None] * coeff - (cross_term * inv_rms**3 / D)[:, None] * residual
    )
    dy_full = lax.all_gather(dresid.astype(jnp.bfloat16), "row", axis=0, tiled=True)
    dhidden = lax.psum_scatter(
        dot_transposed(dy_full, down_block).astype(jnp.bfloat16),
        "col",
        scatter_dimension=0,
        tiled=True,
    ).astype(jnp.float32)
    sigmoid_gate = jax.nn.sigmoid(gate_part)
    gate_grad = dhidden * up_part * sigmoid_gate * (1.0 + gate_part * (1.0 - sigmoid_gate))
    up_grad = dhidden * gate_part * sigmoid_gate
    pre_grad = jnp.concatenate([gate_grad, up_grad], axis=1).astype(jnp.bfloat16)
    input_partial = dot_transposed(lax.all_gather(pre_grad, "col", axis=0, tiled=True), weight)
    placed = lax.dynamic_update_slice_in_dim(jnp.zeros_like(input_partial), dresid, row_start, 0)
    input_grad = lax.psum_scatter(
        (input_partial + placed).astype(jnp.bfloat16),
        ("mp", "row"),
        scatter_dimension=0,
        tiled=True,
    ).astype(jnp.float32)
    return (loss_value, input_grad)


def swap(value, axis, mask, size):
    return lax.ppermute(value, axis, [(i, i ^ mask) for i in range(size)])


def inward(value):
    return lax.ppermute(value, "col", [(0, 1), (3, 2)])


def across(value):
    return lax.ppermute(value, "col", [(1, 2), (2, 1)])


def outward(value):
    return lax.ppermute(value, "col", [(1, 0), (2, 3)])


def reduce_to_ends(near, far):
    passed = far + inward(far)
    gathered = near + across(passed)
    return gathered.astype(F32) + outward(gathered).astype(F32)


def spread_from_ends(value, is_end):
    near = jnp.where(is_end, value, inward(value))
    crossed = across(near)
    return near, crossed, outward(crossed)


def rows_kernel(start, x_ref, w_ref, near_ref, far_ref, held, sems):
    half = x_ref.shape[0] // 2
    count, width = held.shape[0], held.shape[1]
    full, rest = divmod(width, STEP)

    def fetch(g, i, size):
        at = pl.multiple_of(i * STEP, STEP)
        return pltpu.make_async_copy(
            w_ref.at[g, pl.ds(start + at, size), :],
            held.at[g, pl.ds(at, size), :],
            sems.at[g, i],
        )

    def multiply(g, i, size):
        fetch(g, i, size).wait()
        at = pl.multiple_of(i * STEP, STEP)
        block = held[g, pl.ds(at, size), :]
        product = dot_transposed(x_ref[...], block).astype(near_ref.dtype)
        near_ref[g * half : (g + 1) * half, pl.ds(at, size)] = product[:half]
        far_ref[g * half : (g + 1) * half, pl.ds(at, size)] = product[half:]

    for g in range(count):
        lax.fori_loop(0, full, lambda i, c, g=g: (fetch(g, i, STEP).start(), c)[1], 0)
        if rest:
            fetch(g, full, rest).start()
    for g in range(count):
        lax.fori_loop(0, full, lambda i, c, g=g: (multiply(g, i, STEP), c)[1], 0)
        if rest:
            multiply(g, full, rest)


def times_rows(x, w, start, width):
    tokens, depth = x.shape
    count = w.shape[0]
    shape = jax.ShapeDtypeStruct((count * tokens // 2, width), BF16)
    return pl.pallas_call(
        functools.partial(rows_kernel, start),
        out_shape=(shape, shape),
        in_specs=[pl.BlockSpec(memory_space=pltpu.VMEM), pl.BlockSpec(memory_space=pl.ANY)],
        out_specs=(pl.BlockSpec(memory_space=pltpu.VMEM),) * 2,
        scratch_shapes=[
            pltpu.VMEM((count, width, depth), w.dtype),
            pltpu.SemaphoreType.DMA((count, pl.cdiv(width, STEP))),
        ],
        compiler_params=pltpu.CompilerParams(vmem_limit_bytes=VMEM_LIMIT),
        cost_estimate=pl.CostEstimate(
            flops=2 * tokens * depth * width * count,
            bytes_accessed=2 * depth * width * count,
            transcendentals=0,
        ),
    )(x, w)


def columns_kernel(start, first, *refs):
    if first:
        near_ref, far_a_ref, far_b_ref, w_ref, out_ref, held, left, sems = refs
    else:
        acc_ref, near_ref, far_a_ref, far_b_ref, w_ref, out_ref, held, left, sems = refs
    count, width, depth = held.shape
    half = near_ref.shape[0] // count
    steps = depth // WIDE

    def fetch(g, i):
        at = pl.multiple_of(i * WIDE, WIDE)
        return pltpu.make_async_copy(
            w_ref.at[g, pl.ds(start, width), pl.ds(at, WIDE)],
            held.at[g, :, pl.ds(at, WIDE)],
            sems.at[g, i],
        )

    def begin(i, carry):
        for g in range(count):
            fetch(g, i).start()
        return carry

    def multiply(i, carry):
        at = pl.multiple_of(i * WIDE, WIDE)
        total = None if first else acc_ref[:, pl.ds(at, WIDE)]
        for g in range(count):
            fetch(g, i).wait()
            product = jnp.dot(left[g], held[g, :, pl.ds(at, WIDE)], preferred_element_type=F32)
            total = product if total is None else total + product
        out_ref[:, pl.ds(at, WIDE)] = total
        return carry

    lax.fori_loop(0, steps, begin, 0)
    for g in range(count):
        rows = slice(g * half, (g + 1) * half)
        left[g, :half] = near_ref[rows]
        left[g, half:] = far_a_ref[rows] + far_b_ref[rows]
    lax.fori_loop(0, steps, multiply, 0)


def times_columns(acc, near, far_a, far_b, w, start):
    count, _, depth = w.shape
    width = near.shape[1]
    tokens = 2 * near.shape[0] // count
    first = acc is None
    given = (near, far_a, far_b, w) if first else (acc, near, far_a, far_b, w)
    vmem = pl.BlockSpec(memory_space=pltpu.VMEM)
    return pl.pallas_call(
        functools.partial(columns_kernel, start, first),
        out_shape=jax.ShapeDtypeStruct((tokens, depth), F32),
        in_specs=[vmem] * (len(given) - 1) + [pl.BlockSpec(memory_space=pl.ANY)],
        out_specs=vmem,
        scratch_shapes=[
            pltpu.VMEM((count, width, depth), w.dtype),
            pltpu.VMEM((count, tokens, width), BF16),
            pltpu.SemaphoreType.DMA((count, depth // WIDE)),
        ],
        compiler_params=pltpu.CompilerParams(vmem_limit_bytes=VMEM_LIMIT),
        cost_estimate=pl.CostEstimate(
            flops=2 * tokens * depth * width * count,
            bytes_accessed=2 * depth * width * count,
            transcendentals=0,
        ),
    )(*given)


def cuts_of(width, parts):
    total = sum(parts)
    cuts = [STEP * round(width * sum(parts[:k]) / total / STEP) for k in range(len(parts))]
    return list(zip(cuts, [b - a for a, b in zip(cuts, cuts[1:] + [width])]))


def pre_gradient(dhidden, gate, up):
    sigmoid_gate = jax.nn.sigmoid(gate)
    gate_grad = dhidden * up * sigmoid_gate * (1.0 + gate * (1.0 - sigmoid_gate))
    up_grad = dhidden * gate * sigmoid_gate
    return jnp.concatenate([gate_grad, up_grad], axis=0).astype(BF16)


class Overflow:
    def __init__(self, needed, is_end, weight, down, tokens):
        self.needed, self.is_end, self.weight, self.down = needed, is_end, weight, down
        self.half = tokens // 2
        self.count = 6
        self.width = down.shape[0] // self.count

    def block(self, k):
        at = k * self.width
        span = (1, self.width, self.weight.shape[2])
        return (
            lax.dynamic_slice(self.weight, (0, at, 0), span)[0],
            lax.dynamic_slice(self.weight, (1, at, 0), span)[0],
            lax.dynamic_slice_in_dim(self.down, at, self.width, 0),
        )

    def joined(self, near, far_a, far_b):
        far = far_a + far_b
        return [
            jnp.concatenate([near[a : a + self.half], far[a : a + self.half]], axis=0)
            for a in range(0, near.shape[0], self.half)
        ]

    def forward(self, inputs):
        half, features = self.half, inputs.shape[1]

        def step(total, k):
            gate_w, up_w, down = self.block(k)
            gate = dot_transposed(inputs, gate_w).astype(BF16)
            up = dot_transposed(inputs, up_w).astype(BF16)
            sums = reduce_to_ends(
                jnp.concatenate([gate[:half], up[:half]], axis=0),
                jnp.concatenate([gate[half:], up[half:]], axis=0),
            )
            hidden = (jax.nn.silu(sums[:half]) * sums[half:]).astype(BF16)
            (hidden,) = self.joined(*spread_from_ends(hidden, self.is_end))
            return total + jnp.dot(hidden, down, preferred_element_type=F32), sums

        def run():
            total, saved = lax.scan(
                step, jnp.zeros((2 * half, features), F32), jnp.arange(self.count)
            )
            for bit in (1, 2):
                total = total.astype(BF16)
                total = total.astype(F32) + swap(total, "row", bit, 4).astype(F32)
            return total.astype(BF16), saved

        def skip():
            saved = jnp.zeros((self.count, 2 * half, self.width), F32)
            return jnp.zeros((2 * half, features), BF16), saved

        return lax.cond(self.needed, run, skip)

    def backward(self, dy, saved):
        half, features = self.half, dy.shape[1]

        def step(total, at):
            k, sums = at
            gate_w, up_w, down = self.block(k)
            dhidden = dot_transposed(dy, down).astype(BF16)
            dhidden = reduce_to_ends(dhidden[:half], dhidden[half:])
            pre_grad = pre_gradient(dhidden, sums[:half], sums[half:])
            gate_grad, up_grad = self.joined(*spread_from_ends(pre_grad, self.is_end))
            total = total + jnp.dot(gate_grad, gate_w, preferred_element_type=F32)
            return total + jnp.dot(up_grad, up_w, preferred_element_type=F32), None

        def run():
            start = jnp.zeros((2 * half, features), F32)
            return lax.scan(step, start, (jnp.arange(self.count), saved))[0]

        return lax.cond(self.needed, run, lambda: jnp.zeros((2 * half, features), F32))


def line_of_four(
    text_embeds,
    image_embeds,
    offsets,
    lengths,
    loss_mask,
    norm_gain,
    unembed_rows,
    gate_up,
    down_proj,
):
    rows = text_embeds.shape[0]
    img_rows = image_embeds.shape[0]
    tokens = 4 * rows
    eighth = tokens // 8
    seq_count = offsets.shape[0]
    extra = tokens // 5
    main = tokens - extra
    model_id = lax.axis_index("mp")
    row_id = lax.axis_index("row")
    col_id = lax.axis_index("col")
    is_policy = model_id == 0
    chip_bit = row_id // 2
    core_bit = row_id % 2
    is_end = (col_id == 0) | (col_id == 3)
    right = (col_id >= 2).astype(jnp.int32)

    def iota(shape, dim):
        return lax.broadcasted_iota(jnp.int32, shape, dim)

    def by_seq(seq, values):
        found = jnp.zeros(seq.shape, values.dtype)
        for k in range(seq_count):
            found = jnp.where(seq == k, values[k], found)
        return found

    lanes = iota((1, tokens), 1)
    mask = lax.dynamic_update_slice(
        jnp.zeros((1, tokens), F32), (loss_mask == 1).astype(F32)[None], (0, row_id * rows)
    )
    mask = mask + swap(mask, "row", 2, 4)
    mask = mask + swap(mask, "row", 1, 4)
    scored = jnp.where(lanes % SEQ < by_seq(lanes // SEQ, lengths), mask, 0.0)
    square = (tokens, tokens)
    upto = (iota(square, 0) <= iota(square, 1)).astype(BF16)
    rank = jnp.dot(scored.astype(BF16), upto, preferred_element_type=F32).astype(jnp.int32)
    overflow = rank[0, tokens - 1] > main
    place = iota(square, 0)

    def near_first(within, span):
        half = span // 2
        return ((within // half) ^ right) * half + within % half

    slot = jnp.where(
        place < main, near_first(place, main), main + near_first(place - main, extra)
    )
    chosen = ((rank == slot + 1) & (scored > 0.5)).astype(BF16)

    own = jnp.concatenate([text_embeds, image_embeds], axis=0)
    over_x = swap(own, "row", 2, 4)
    over_y = swap(image_embeds, "mp", 1, 2)
    over_xy = swap(image_embeds, ("mp", "row"), 6, 8)
    mine = jnp.concatenate([own, over_x, over_y, over_xy], axis=0)
    both = jnp.concatenate([mine, swap(mine, "row", 1, 4)], axis=0)
    core_span = mine.shape[0]
    grid = (tokens, 2 * core_span)
    token = iota(grid, 0)
    position = token % SEQ
    seq = token // SEQ
    first = by_seq(seq, offsets)
    inside = (position >= first) & (position < first + IMG)
    block = token // rows
    text_src = (
        ((block % 2) ^ core_bit) * core_span
        + ((block // 2) ^ chip_bit) * (rows + img_rows)
        + token % rows
    )
    image = seq * IMG + position - first
    holder = image // img_rows
    img_chip = ((holder // 2) % 2) ^ chip_bit
    img_src = (
        ((holder % 2) ^ core_bit) * core_span
        + jnp.where(
            (holder // 4) == model_id,
            img_chip * (rows + img_rows) + rows,
            2 * (rows + img_rows) + img_chip * img_rows,
        )
        + image % img_rows
    )
    source = jnp.where(inside, img_src, text_src)
    held_at = (source == iota(grid, 1)).astype(BF16)
    pick = jnp.dot(chosen, held_at, preferred_element_type=F32).astype(BF16)
    inputs = jnp.dot(pick, both, preferred_element_type=F32).astype(BF16)
    weight = jnp.transpose(gate_up[0], (1, 2, 0))
    features = weight.shape[2]
    rest = Overflow(overflow, is_end, weight, down_proj[0], extra)
    rest_out, rest_saved = rest.forward(inputs[main:])

    cuts = cuts_of(gate_up.shape[3], FORWARD)
    half = main // 2
    saved = []
    out_partial = None
    for start, width in cuts:
        near, far = times_rows(inputs[:main], weight, start, width)
        sums = reduce_to_ends(near, far)
        gate, up = sums[:half], sums[half:]
        saved.append((gate, up))
        hidden = (jax.nn.silu(gate) * up).astype(BF16)
        spread = spread_from_ends(hidden, is_end)
        out_partial = times_columns(out_partial, *spread, down_proj, start)

    target_own = unembed_rows[0]
    target = jnp.concatenate([target_own, swap(target_own, "row", 2, 4)], axis=0)
    target = jnp.concatenate([target, swap(target, "row", 1, 4)], axis=0)
    token = iota(square, 0)
    block = token // rows
    source = (
        ((block % 2) ^ core_bit) * (2 * rows) + ((block // 2) ^ chip_bit) * rows + token % rows
    )
    held_at = (source == iota(square, 1)).astype(BF16)
    pick = jnp.dot(chosen, held_at, preferred_element_type=F32).astype(BF16)
    target = jnp.dot(pick, target, preferred_element_type=F32)
    coeff = norm_gain[0].astype(F32)[None, :] * target

    lower, upper = out_partial[:half], out_partial[half:]
    keep = jnp.where(core_bit == 0, lower, upper)
    give = jnp.where(core_bit == 0, upper, lower)
    pair = (keep + swap(give.astype(BF16), "row", 1, 4).astype(F32)).astype(BF16)
    summed = (pair.astype(F32) + swap(pair, "row", 2, 4).astype(F32)).astype(BF16)
    other = swap(summed, "row", 1, 4)
    block_out = jnp.concatenate(
        [
            jnp.where(core_bit == 0, summed, other),
            jnp.where(core_bit == 0, other, summed),
            rest_out,
        ],
        axis=0,
    )
    residual = inputs.astype(F32) + block_out.astype(F32)

    exact = functools.partial(
        lax.dot_general, precision=lax.Precision.HIGHEST, preferred_element_type=F32
    )
    chosen32 = chosen.astype(F32)
    sums = jnp.concatenate(
        [
            jnp.sum(residual * residual, axis=1, keepdims=True),
            jnp.sum(residual * coeff, axis=1, keepdims=True),
        ],
        axis=1,
    )
    sums = exact(sums, chosen32, (((0,), (0,)), ((), ())))
    sums = sums + swap(sums, "col", 1, 4)
    sums = sums + swap(sums, "col", 2, 4)
    theirs = swap(sums, "mp", 1, 2)

    def scores(of):
        return scored * of[1:] * lax.rsqrt(of[:1] / D + norm_eps)

    ahead = jnp.where(is_policy, scores(sums) - scores(theirs), scores(theirs) - scores(sums))
    seq_from, seq_to = iota(square, 0) // SEQ, iota(square, 1) // SEQ
    sign = jnp.where(seq_from % 2 == 0, 1.0, -1.0)
    paired = jnp.where(seq_from // 2 == seq_to // 2, sign, 0.0)
    margin = exact(ahead, paired, (((1,), (0,)), ((), ())))
    loss_value = jnp.sum(jax.nn.softplus(-dpo_beta * margin)) / tokens
    dmargin = -dpo_beta * jax.nn.sigmoid(-dpo_beta * margin) / (seq_count // 2)
    dscore = jnp.where((lanes // SEQ) % 2 == 0, dmargin, -dmargin)
    dscore = jnp.where(is_policy, scored * dscore, 0.0)
    inv_rms = lax.rsqrt(sums[:1] / D + norm_eps)
    slopes = jnp.concatenate(
        [dscore * inv_rms, dscore * (sums[1:] * inv_rms**3 / D)], axis=0
    )
    slopes = exact(chosen32, slopes, (((1,), (1,)), ((), ())))
    dresid = slopes[:, :1] * coeff - slopes[:, 1:] * residual
    dy = dresid.astype(BF16)

    rest_grad = rest.backward(dy[main:], rest_saved)
    grad_partial = jnp.where(row_id == 0, dresid[:main], 0.0)
    for k, (start, width) in enumerate(cuts):
        near, far = times_rows(dy[:main], down_proj, start, width)
        dhidden = reduce_to_ends(near, far)
        spread = spread_from_ends(pre_gradient(dhidden, *saved[k]), is_end)
        grad_partial = times_columns(grad_partial, *spread, weight, start)

    rest_grad = rest_grad + jnp.where(row_id == 0, dresid[main:], 0.0)
    grads = jnp.concatenate([grad_partial, rest_grad], axis=0)
    within = iota(square, 0) % (tokens // 2)
    block = within // eighth
    token = (
        iota(square, 0) // (tokens // 2) * (tokens // 2)
        + ((block % 2) * 2 + block // 2) * eighth
        + within % eighth
    )
    placed = lax.dot_general(
        (token == iota(square, 1)).astype(BF16),
        chosen,
        (((1,), (1,)), ((), ())),
        preferred_element_type=F32,
    ).astype(BF16)
    high = grads.astype(BF16)
    low = (grads - high.astype(F32)).astype(BF16)
    grads = jnp.dot(placed, high, preferred_element_type=F32) + jnp.dot(
        placed, low, preferred_element_type=F32
    )

    folded = grads.reshape(2, 2, 2 * eighth, features)
    keep = jnp.where(core_bit == 0, folded[:, 0], folded[:, 1])
    give = jnp.where(core_bit == 0, folded[:, 1], folded[:, 0])
    pair = keep + swap(give.astype(BF16), "row", 1, 4).astype(F32)
    folded = pair.reshape(2, 2, eighth, features)
    keep = jnp.where(chip_bit == 0, folded[:, 0], folded[:, 1])
    give = jnp.where(chip_bit == 0, folded[:, 1], folded[:, 0])
    total = keep + swap(give.astype(BF16), "row", 2, 4).astype(F32)
    sent = lax.ppermute(total[1].astype(BF16), "mp", [(0, 1)])
    input_grad = jnp.where(is_policy, total[0], sent.astype(F32))
    return (loss_value, input_grad)


def solution(mesh):
    in_specs = (
        P("row", "col"),
        P(("mp", "row"), "col"),
        P(),
        P(),
        P("row"),
        P("mp", "col"),
        P("mp", "row", "col"),
        P("mp", "col", None, "row"),
        P("mp", "row", "col"),
    )
    out_specs = (P(), P(("mp", "row"), "col"))
    sizes = dict(mesh.shape)
    if not (sizes["mp"] == 2 and sizes["row"] == 4 and sizes["col"] == 4):
        return jax.shard_map(
            general, mesh=mesh, in_specs=in_specs, out_specs=out_specs, check_vma=False
        )

    return jax.shard_map(line_of_four, mesh=mesh, in_specs=in_specs, out_specs=out_specs, check_vma=False)
```

```python
import functools

import jax
import jax.numpy as jnp
from jax import lax
from jax.experimental import pallas as pl
from jax.experimental.pallas import tpu as pltpu
from jax.sharding import PartitionSpec as P

D = 8192
SEQ = 40
IMG = 16


dpo_beta = 0.1
norm_eps = 1e-06

FORWARD = (6, 7, 8, 7.875)
STEP = 256
WIDE = 512
VMEM_LIMIT = 28 * 1024 * 1024
BF16 = jnp.bfloat16
F32 = jnp.float32


def place_images(text_rows, images, offsets):
    tokens = text_rows.shape[0]
    global_pos = jnp.arange(tokens, dtype=jnp.int32)
    position = global_pos % SEQ
    seq_id = global_pos // SEQ
    first_img = offsets[seq_id]
    inside = (position >= first_img) & (position < first_img + IMG)
    source = jnp.clip(seq_id * IMG + position - first_img, 0, images.shape[0] - 1)
    return jnp.where(inside[:, None], jnp.take(images, source, axis=0), text_rows)


def dpo_terms(totals):
    policy = totals[0]
    frozen = totals[1]
    margin = policy[0::2] - frozen[0::2] - (policy[1::2] - frozen[1::2])
    loss_value = jnp.mean(jax.nn.softplus(-dpo_beta * margin))
    dmargin = -dpo_beta * jax.nn.sigmoid(-dpo_beta * margin) / margin.shape[0]
    return (loss_value, dmargin)


def dot_transposed(left, right):
    return lax.dot_general(
        left, right, (((1,), (1,)), ((), ())), preferred_element_type=jnp.float32
    )


def general(
    text_embeds,
    image_embeds,
    offsets,
    lengths,
    loss_mask,
    norm_gain,
    unembed_rows,
    gate_up,
    down_proj,
):
    text_full = lax.all_gather(text_embeds, "row", axis=0, tiled=True)
    images = lax.all_gather(image_embeds, ("mp", "row"), axis=0, tiled=True)
    inputs = place_images(text_full, images, offsets)
    tokens = inputs.shape[0]
    local_rows = tokens // lax.axis_size("row")
    hidden_width = gate_up.shape[3]
    weight = gate_up[0].reshape(gate_up.shape[1], 2 * hidden_width)
    down_block = down_proj[0]
    row_start = lax.axis_index("row") * local_rows
    pre_sums = lax.psum_scatter(
        jnp.dot(inputs, weight, preferred_element_type=jnp.float32).astype(jnp.bfloat16),
        "col",
        scatter_dimension=0,
        tiled=True,
    ).astype(jnp.float32)
    gate_part = pre_sums[:, :hidden_width]
    up_part = pre_sums[:, hidden_width:]
    hidden = (jax.nn.silu(gate_part) * up_part).astype(jnp.bfloat16)
    out_partial = jnp.dot(
        lax.all_gather(hidden, "col", axis=0, tiled=True),
        down_block,
        preferred_element_type=jnp.float32,
    )
    block_out = lax.psum_scatter(
        out_partial.astype(jnp.bfloat16), "row", scatter_dimension=0, tiled=True
    ).astype(jnp.float32)
    own_rows = lax.dynamic_slice_in_dim(inputs, row_start, local_rows, 0)
    residual = own_rows.astype(jnp.float32) + block_out
    coeff = norm_gain[0].astype(jnp.float32)[None, :] * unembed_rows[0].astype(jnp.float32)
    squares, cross_term = lax.psum(
        (jnp.sum(residual * residual, axis=1), jnp.sum(residual * coeff, axis=1)), "col"
    )
    inv_rms = lax.rsqrt(squares / D + norm_eps)
    tok_score = cross_term * inv_rms
    global_pos = row_start + jnp.arange(local_rows, dtype=jnp.int32)
    position = global_pos % SEQ
    seq_id = global_pos // SEQ
    scored = ((position < lengths[seq_id]) & (loss_mask == 1)).astype(jnp.float32)
    seq_count = offsets.shape[0]
    onehot = (seq_id[:, None] == jnp.arange(seq_count, dtype=jnp.int32)[None, :]).astype(
        jnp.float32
    )
    seq_part = jnp.dot(scored * tok_score, onehot, precision=lax.Precision.HIGHEST)
    model_id = lax.axis_index("mp")
    score_slots = (jnp.arange(2, dtype=jnp.int32) == model_id).astype(jnp.float32)[
        :, None
    ] * seq_part[None, :]
    totals = lax.psum(score_slots, ("mp", "row"))
    loss_value, dmargin = dpo_terms(totals)
    policy_flag = (model_id == 0).astype(jnp.float32)
    seq_grad = policy_flag * jnp.stack([dmargin, -dmargin], axis=1).reshape(seq_count)
    dscore = scored * jnp.dot(onehot, seq_grad, precision=lax.Precision.HIGHEST)
    dresid = dscore[:, None] * (
        inv_rms[:, None] * coeff - (cross_term * inv_rms**3 / D)[:, None] * residual
    )
    dy_full = lax.all_gather(dresid.astype(jnp.bfloat16), "row", axis=0, tiled=True)
    dhidden = lax.psum_scatter(
        dot_transposed(dy_full, down_block).astype(jnp.bfloat16),
        "col",
        scatter_dimension=0,
        tiled=True,
    ).astype(jnp.float32)
    sigmoid_gate = jax.nn.sigmoid(gate_part)
    gate_grad = dhidden * up_part * sigmoid_gate * (1.0 + gate_part * (1.0 - sigmoid_gate))
    up_grad = dhidden * gate_part * sigmoid_gate
    pre_grad = jnp.concatenate([gate_grad, up_grad], axis=1).astype(jnp.bfloat16)
    input_partial = dot_transposed(lax.all_gather(pre_grad, "col", axis=0, tiled=True), weight)
    placed = lax.dynamic_update_slice_in_dim(jnp.zeros_like(input_partial), dresid, row_start, 0)
    input_grad = lax.psum_scatter(
        (input_partial + placed).astype(jnp.bfloat16),
        ("mp", "row"),
        scatter_dimension=0,
        tiled=True,
    ).astype(jnp.float32)
    return (loss_value, input_grad)


def swap(value, axis, mask, size):
    return lax.ppermute(value, axis, [(i, i ^ mask) for i in range(size)])


def inward(value):
    return lax.ppermute(value, "col", [(0, 1), (3, 2)])


def across(value):
    return lax.ppermute(value, "col", [(1, 2), (2, 1)])


def outward(value):
    return lax.ppermute(value, "col", [(1, 0), (2, 3)])


def reduce_to_ends(near, far):
    passed = far + inward(far)
    gathered = near + across(passed)
    return gathered.astype(F32) + outward(gathered).astype(F32)


def spread_from_ends(value, is_end):
    near = jnp.where(is_end, value, inward(value))
    crossed = across(near)
    return near, crossed, outward(crossed)


def rows_kernel(start, x_ref, w_ref, near_ref, far_ref, held, sems):
    half = x_ref.shape[0] // 2
    count, width = held.shape[0], held.shape[1]
    full, rest = divmod(width, STEP)

    def fetch(g, i, size):
        at = pl.multiple_of(i * STEP, STEP)
        return pltpu.make_async_copy(
            w_ref.at[g, pl.ds(start + at, size), :],
            held.at[g, pl.ds(at, size), :],
            sems.at[g, i],
        )

    def multiply(g, i, size):
        fetch(g, i, size).wait()
        at = pl.multiple_of(i * STEP, STEP)
        block = held[g, pl.ds(at, size), :]
        product = dot_transposed(x_ref[...], block).astype(near_ref.dtype)
        near_ref[g * half : (g + 1) * half, pl.ds(at, size)] = product[:half]
        far_ref[g * half : (g + 1) * half, pl.ds(at, size)] = product[half:]

    for g in range(count):
        lax.fori_loop(0, full, lambda i, c, g=g: (fetch(g, i, STEP).start(), c)[1], 0)
        if rest:
            fetch(g, full, rest).start()
    for g in range(count):
        lax.fori_loop(0, full, lambda i, c, g=g: (multiply(g, i, STEP), c)[1], 0)
        if rest:
            multiply(g, full, rest)


def times_rows(x, w, start, width):
    tokens, depth = x.shape
    count = w.shape[0]
    shape = jax.ShapeDtypeStruct((count * tokens // 2, width), BF16)
    return pl.pallas_call(
        functools.partial(rows_kernel, start),
        out_shape=(shape, shape),
        in_specs=[pl.BlockSpec(memory_space=pltpu.VMEM), pl.BlockSpec(memory_space=pl.ANY)],
        out_specs=(pl.BlockSpec(memory_space=pltpu.VMEM),) * 2,
        scratch_shapes=[
            pltpu.VMEM((count, width, depth), w.dtype),
            pltpu.SemaphoreType.DMA((count, pl.cdiv(width, STEP))),
        ],
        compiler_params=pltpu.CompilerParams(vmem_limit_bytes=VMEM_LIMIT),
        cost_estimate=pl.CostEstimate(
            flops=2 * tokens * depth * width * count,
            bytes_accessed=2 * depth * width * count,
            transcendentals=0,
        ),
    )(x, w)


def columns_kernel(start, first, *refs):
    if first:
        near_ref, far_a_ref, far_b_ref, w_ref, out_ref, held, left, sems = refs
    else:
        acc_ref, near_ref, far_a_ref, far_b_ref, w_ref, out_ref, held, left, sems = refs
    count, width, depth = held.shape
    half = near_ref.shape[0] // count
    steps = depth // WIDE

    def fetch(g, i):
        at = pl.multiple_of(i * WIDE, WIDE)
        return pltpu.make_async_copy(
            w_ref.at[g, pl.ds(start, width), pl.ds(at, WIDE)],
            held.at[g, :, pl.ds(at, WIDE)],
            sems.at[g, i],
        )

    def begin(i, carry):
        for g in range(count):
            fetch(g, i).start()
        return carry

    def multiply(i, carry):
        at = pl.multiple_of(i * WIDE, WIDE)
        total = None if first else acc_ref[:, pl.ds(at, WIDE)]
        for g in range(count):
            fetch(g, i).wait()
            product = jnp.dot(left[g], held[g, :, pl.ds(at, WIDE)], preferred_element_type=F32)
            total = product if total is None else total + product
        out_ref[:, pl.ds(at, WIDE)] = total
        return carry

    lax.fori_loop(0, steps, begin, 0)
    for g in range(count):
        rows = slice(g * half, (g + 1) * half)
        left[g, :half] = near_ref[rows]
        left[g, half:] = far_a_ref[rows] + far_b_ref[rows]
    lax.fori_loop(0, steps, multiply, 0)


def times_columns(acc, near, far_a, far_b, w, start):
    count, _, depth = w.shape
    width = near.shape[1]
    tokens = 2 * near.shape[0] // count
    first = acc is None
    given = (near, far_a, far_b, w) if first else (acc, near, far_a, far_b, w)
    vmem = pl.BlockSpec(memory_space=pltpu.VMEM)
    return pl.pallas_call(
        functools.partial(columns_kernel, start, first),
        out_shape=jax.ShapeDtypeStruct((tokens, depth), F32),
        in_specs=[vmem] * (len(given) - 1) + [pl.BlockSpec(memory_space=pl.ANY)],
        out_specs=vmem,
        scratch_shapes=[
            pltpu.VMEM((count, width, depth), w.dtype),
            pltpu.VMEM((count, tokens, width), BF16),
            pltpu.SemaphoreType.DMA((count, depth // WIDE)),
        ],
        compiler_params=pltpu.CompilerParams(vmem_limit_bytes=VMEM_LIMIT),
        cost_estimate=pl.CostEstimate(
            flops=2 * tokens * depth * width * count,
            bytes_accessed=2 * depth * width * count,
            transcendentals=0,
        ),
    )(*given)


def cuts_of(width, parts):
    total = sum(parts)
    cuts = [STEP * round(width * sum(parts[:k]) / total / STEP) for k in range(len(parts))]
    return list(zip(cuts, [b - a for a, b in zip(cuts, cuts[1:] + [width])]))


def pre_gradient(dhidden, gate, up):
    sigmoid_gate = jax.nn.sigmoid(gate)
    gate_grad = dhidden * up * sigmoid_gate * (1.0 + gate * (1.0 - sigmoid_gate))
    up_grad = dhidden * gate * sigmoid_gate
    return jnp.concatenate([gate_grad, up_grad], axis=0).astype(BF16)


def count_of(value, step, most):
    found = jnp.zeros(value.shape, jnp.int32)
    for k in range(1, most):
        found = found + jnp.where(value >= k * step, 1, 0)
    return found


def by_seq(seq, values_ref):
    found = jnp.zeros(seq.shape, jnp.int32)
    for k in range(values_ref.shape[0]):
        found = jnp.where(seq == k, values_ref[k], found)
    return found


def one_hot(test):
    return jnp.where(test, 1.0, 0.0).astype(BF16)


def place_kernel(
    rows, img_rows, extra, offsets_ref, lengths_ref, mine_ref, other_ref,
    inputs_ref, chosen_ref, scored_ref, rank_ref,
):
    tokens = inputs_ref.shape[0]
    main = tokens - extra
    seq_count = offsets_ref.shape[0]
    row_id = lax.axis_index("row")
    model_id = lax.axis_index("mp")
    right = jnp.where(lax.axis_index("col") >= 2, 1, 0)
    chip_bit = jnp.where(row_id >= 2, 1, 0)
    core_bit = row_id - 2 * chip_bit

    def iota(shape, dim):
        return lax.broadcasted_iota(jnp.int32, shape, dim)

    def differ(a, b):
        return jnp.where(a == b, 0, 1)

    own = rows + img_rows + 8
    mask = jnp.zeros((1, tokens), F32)
    for core in range(2):
        for chip in range(2):
            at = (chip + 1) * own - 8
            piece = (mine_ref if core == 0 else other_ref)[at : at + 8, :rows]
            held = 2 * differ(chip_bit, chip) + differ(core_bit, core)
            spread = one_hot(
                iota((rows, tokens), 1) == iota((rows, tokens), 0) + held * rows
            )
            mask = mask + jnp.dot(piece, spread, preferred_element_type=F32)[:1]
    lanes = iota((1, tokens), 1)
    seq = count_of(lanes, SEQ, seq_count)
    scored = jnp.where(lanes - seq * SEQ < by_seq(seq, lengths_ref), mask, 0.0)
    square = (tokens, tokens)
    upto = one_hot(iota(square, 0) <= iota(square, 1))
    rank = jnp.dot(scored.astype(BF16), upto, preferred_element_type=F32)
    scored_ref[...] = scored
    rank_ref[...] = rank

    def near_first(within, span):
        upper = jnp.where(within >= span // 2, 1, 0)
        return differ(upper, right) * (span // 2) + within - upper * (span // 2)

    place = iota(square, 0)
    slot = jnp.where(
        place < main, near_first(place, main), main + near_first(place - main, extra)
    )
    matched = jnp.where(rank.astype(jnp.int32) == slot + 1, scored, 0.0)
    chosen = matched.astype(BF16)
    chosen_ref[...] = chosen

    span = mine_ref.shape[0]
    grid = (tokens, span)
    token = iota(grid, 0)
    seq = count_of(token, SEQ, seq_count)
    within = token - seq * SEQ - by_seq(seq, offsets_ref)
    inside = (within >= 0) & (within < IMG)
    block = count_of(token, rows, 4)
    chip = jnp.where(block >= 2, 1, 0)
    core = block - 2 * chip
    text_core = differ(core, core_bit)
    text_at = differ(chip, chip_bit) * own + token - block * rows
    image = seq * IMG + within
    holder = count_of(image, img_rows, 8)
    model = jnp.where(holder >= 4, 1, 0)
    chip = jnp.where(holder - 4 * model >= 2, 1, 0)
    core = holder - 4 * model - 2 * chip
    chip = differ(chip, chip_bit)
    img_core = differ(core, core_bit)
    img_at = image - holder * img_rows + jnp.where(
        model == model_id, chip * own + rows, 2 * own + chip * img_rows
    )
    at = jnp.where(inside, img_at, text_at)
    side = jnp.where(inside, img_core, text_core)
    column = iota(grid, 1)
    total = None
    for core, held_ref in ((0, mine_ref), (1, other_ref)):
        held = one_hot((at == column) & (side == core))
        pick = jnp.dot(chosen, held, preferred_element_type=F32).astype(BF16)
        part = jnp.dot(pick, held_ref[...], preferred_element_type=F32)
        total = part if total is None else total + part
    inputs_ref[...] = total.astype(BF16)


def sums_kernel(
    inputs_ref, summed_ref, other_ref, rest_ref, coeff_ref, chosen_ref, residual_ref, sums_ref
):
    half = summed_ref.shape[0]
    first = lax.rem(lax.axis_index("row"), 2) == 0
    summed, other = summed_ref[...].astype(F32), other_ref[...].astype(F32)
    spans = (
        (0, half, jnp.where(first, summed, other)),
        (half, 2 * half, jnp.where(first, other, summed)),
        (2 * half, inputs_ref.shape[0], rest_ref[...].astype(F32)),
    )
    squares = jnp.zeros((1, chosen_ref.shape[1]), F32)
    cross = jnp.zeros((1, chosen_ref.shape[1]), F32)
    for a, b, block_out in spans:
        residual = inputs_ref[a:b, :].astype(F32) + block_out
        residual_ref[a:b, :] = residual
        chosen = chosen_ref[a:b, :].astype(F32)
        square = jnp.sum(residual * residual, axis=1, keepdims=True)
        product = jnp.sum(residual * coeff_ref[a:b, :], axis=1, keepdims=True)
        squares = squares + jnp.sum(chosen * square, axis=0, keepdims=True)
        cross = cross + jnp.sum(chosen * product, axis=0, keepdims=True)
    sums_ref[0:1, :] = squares
    sums_ref[1:2, :] = cross


def score_kernel(
    seq_count, sums_ref, theirs_ref, scored_ref, chosen_ref, coeff_ref, residual_ref,
    margin_ref, dy_ref, dy_rest_ref, grad_ref, grad_rest_ref,
):
    tokens = scored_ref.shape[1]
    is_policy = lax.axis_index("mp") == 0
    scored = scored_ref[...]

    def scores(ref):
        return scored * ref[1:2, :] * lax.rsqrt(ref[0:1, :] / D + norm_eps)

    ahead = scores(sums_ref) - scores(theirs_ref)
    ahead = jnp.where(is_policy, ahead, -ahead)
    seq = count_of(lax.broadcasted_iota(jnp.int32, (1, tokens), 1), SEQ, seq_count)
    margin = jnp.zeros((1, tokens), F32)
    sign = jnp.zeros((1, tokens), F32)
    for k in range(0, seq_count, 2):
        chosen_sum = jnp.sum(jnp.where(seq == k, ahead, 0.0), axis=1, keepdims=True)
        rejected_sum = jnp.sum(jnp.where(seq == k + 1, ahead, 0.0), axis=1, keepdims=True)
        margin = jnp.where((seq == k) | (seq == k + 1), chosen_sum - rejected_sum, margin)
        sign = jnp.where(seq == k, 1.0, jnp.where(seq == k + 1, -1.0, sign))
    margin_ref[...] = margin
    dmargin = -dpo_beta * jax.nn.sigmoid(-dpo_beta * margin) / (seq_count // 2)
    dscore = jnp.where(is_policy, scored * sign * dmargin, 0.0)
    inv_rms = lax.rsqrt(sums_ref[0:1, :] / D + norm_eps)
    along = dscore * inv_rms
    back = dscore * (sums_ref[1:2, :] * inv_rms * inv_rms * inv_rms / D)
    adds = lax.axis_index("row") == 0
    main = dy_ref.shape[0]
    for a, b, dy_out, grad_out in (
        (0, main, dy_ref, grad_ref),
        (main, tokens, dy_rest_ref, grad_rest_ref),
    ):
        chosen = chosen_ref[a:b, :].astype(F32)
        by_coeff = jnp.sum(chosen * along, axis=1, keepdims=True)
        by_residual = jnp.sum(chosen * back, axis=1, keepdims=True)
        dresid = by_coeff * coeff_ref[a:b, :] - by_residual * residual_ref[a:b, :]
        dy_out[...] = dresid.astype(BF16)
        grad_out[...] = jnp.where(adds, dresid, 0.0)


class Overflow:
    def __init__(self, needed, is_end, weight, down, tokens):
        self.needed, self.is_end, self.weight, self.down = needed, is_end, weight, down
        self.half = tokens // 2
        self.count = 6
        self.width = down.shape[0] // self.count

    def block(self, k):
        at = k * self.width
        span = (1, self.width, self.weight.shape[2])
        return (
            lax.dynamic_slice(self.weight, (0, at, 0), span)[0],
            lax.dynamic_slice(self.weight, (1, at, 0), span)[0],
            lax.dynamic_slice_in_dim(self.down, at, self.width, 0),
        )

    def joined(self, near, far_a, far_b):
        far = far_a + far_b
        return [
            jnp.concatenate([near[a : a + self.half], far[a : a + self.half]], axis=0)
            for a in range(0, near.shape[0], self.half)
        ]

    def forward(self, inputs):
        half, features = self.half, inputs.shape[1]

        def step(total, k):
            gate_w, up_w, down = self.block(k)
            gate = dot_transposed(inputs, gate_w).astype(BF16)
            up = dot_transposed(inputs, up_w).astype(BF16)
            sums = reduce_to_ends(
                jnp.concatenate([gate[:half], up[:half]], axis=0),
                jnp.concatenate([gate[half:], up[half:]], axis=0),
            )
            hidden = (jax.nn.silu(sums[:half]) * sums[half:]).astype(BF16)
            (hidden,) = self.joined(*spread_from_ends(hidden, self.is_end))
            return total + jnp.dot(hidden, down, preferred_element_type=F32), sums

        def run():
            total, saved = lax.scan(
                step, jnp.zeros((2 * half, features), F32), jnp.arange(self.count)
            )
            for bit in (1, 2):
                total = total.astype(BF16)
                total = total.astype(F32) + swap(total, "row", bit, 4).astype(F32)
            return total.astype(BF16), saved

        def skip():
            saved = jnp.zeros((self.count, 2 * half, self.width), F32)
            return jnp.zeros((2 * half, features), BF16), saved

        return lax.cond(self.needed, run, skip)

    def backward(self, dy, saved):
        half, features = self.half, dy.shape[1]

        def step(total, at):
            k, sums = at
            gate_w, up_w, down = self.block(k)
            dhidden = dot_transposed(dy, down).astype(BF16)
            dhidden = reduce_to_ends(dhidden[:half], dhidden[half:])
            pre_grad = pre_gradient(dhidden, sums[:half], sums[half:])
            gate_grad, up_grad = self.joined(*spread_from_ends(pre_grad, self.is_end))
            total = total + jnp.dot(gate_grad, gate_w, preferred_element_type=F32)
            return total + jnp.dot(up_grad, up_w, preferred_element_type=F32), None

        def run():
            start = jnp.zeros((2 * half, features), F32)
            return lax.scan(step, start, (jnp.arange(self.count), saved))[0]

        return lax.cond(self.needed, run, lambda: jnp.zeros((2 * half, features), F32))


def line_of_four(
    text_embeds,
    image_embeds,
    offsets,
    lengths,
    loss_mask,
    norm_gain,
    unembed_rows,
    gate_up,
    down_proj,
):
    rows = text_embeds.shape[0]
    img_rows = image_embeds.shape[0]
    tokens = 4 * rows
    eighth = tokens // 8
    seq_count = offsets.shape[0]
    extra = tokens // 5
    main = tokens - extra
    model_id = lax.axis_index("mp")
    row_id = lax.axis_index("row")
    col_id = lax.axis_index("col")
    is_policy = model_id == 0
    chip_bit = row_id // 2
    core_bit = row_id % 2
    is_end = (col_id == 0) | (col_id == 3)

    def iota(shape, dim):
        return lax.broadcasted_iota(jnp.int32, shape, dim)

    mask = jnp.pad(
        (loss_mask == 1).astype(BF16)[None], ((0, 7), (0, text_embeds.shape[1] - rows))
    )
    own = jnp.concatenate([text_embeds, image_embeds, mask], axis=0)
    over_x = swap(own, "row", 2, 4)
    over_y = swap(image_embeds, "mp", 1, 2)
    over_xy = swap(image_embeds, ("mp", "row"), 6, 8)
    mine = jnp.concatenate([own, over_x, over_y, over_xy], axis=0)
    other = swap(mine, "row", 1, 4)
    smem, vmem = pl.BlockSpec(memory_space=pltpu.SMEM), pl.BlockSpec(memory_space=pltpu.VMEM)
    inputs, chosen, scored, rank = pl.pallas_call(
        functools.partial(place_kernel, rows, img_rows, extra),
        out_shape=(
            jax.ShapeDtypeStruct((tokens, text_embeds.shape[1]), BF16),
            jax.ShapeDtypeStruct((tokens, tokens), BF16),
            jax.ShapeDtypeStruct((1, tokens), F32),
            jax.ShapeDtypeStruct((1, tokens), F32),
        ),
        in_specs=[smem, smem] + [vmem] * 2,
        out_specs=(vmem,) * 4,
        name="place",
    )(offsets, lengths, mine, other)
    overflow = rank[0, tokens - 1] > main
    square = (tokens, tokens)
    lanes = iota((1, tokens), 1)
    weight = jnp.transpose(gate_up[0], (1, 2, 0))
    features = weight.shape[2]
    rest = Overflow(overflow, is_end, weight, down_proj[0], extra)
    rest_out, rest_saved = rest.forward(inputs[main:])

    target_own = unembed_rows[0]
    over_x = swap(target_own, "row", 2, 4)
    target = jnp.concatenate([target_own, over_x], axis=0)
    over_core = swap(target, "row", 1, 4)
    target = jnp.concatenate([target, over_core], axis=0)
    token = iota(square, 0)
    block = token // rows
    source = (
        ((block % 2) ^ core_bit) * (2 * rows) + ((block // 2) ^ chip_bit) * rows + token % rows
    )
    held_at = (source == iota(square, 1)).astype(BF16)
    pick = jnp.dot(chosen, held_at, preferred_element_type=F32).astype(BF16)
    target = jnp.dot(pick, target, preferred_element_type=F32)
    coeff = norm_gain[0].astype(F32)[None, :] * target

    cuts = cuts_of(gate_up.shape[3], FORWARD)
    half = main // 2
    saved = []
    out_partial = None
    for start, width in cuts:
        near, far = times_rows(inputs[:main], weight, start, width)
        sums = reduce_to_ends(near, far)
        gate, up = sums[:half], sums[half:]
        saved.append((gate, up))
        hidden = (jax.nn.silu(gate) * up).astype(BF16)
        spread = spread_from_ends(hidden, is_end)
        out_partial = times_columns(out_partial, *spread, down_proj, start)

    lower, upper = out_partial[:half], out_partial[half:]
    keep = jnp.where(core_bit == 0, lower, upper)
    give = jnp.where(core_bit == 0, upper, lower)
    pair = (keep + swap(give.astype(BF16), "row", 1, 4).astype(F32)).astype(BF16)
    summed = (pair.astype(F32) + swap(pair, "row", 2, 4).astype(F32)).astype(BF16)
    other = swap(summed, "row", 1, 4)
    residual, sums = pl.pallas_call(
        sums_kernel,
        out_shape=(
            jax.ShapeDtypeStruct((tokens, features), F32),
            jax.ShapeDtypeStruct((2, tokens), F32),
        ),
        in_specs=[vmem] * 6,
        out_specs=(vmem,) * 2,
        compiler_params=pltpu.CompilerParams(vmem_limit_bytes=24 * 1024 * 1024),
        name="sums",
    )(inputs, summed, other, rest_out, coeff, chosen)

    sums = (sums + swap(sums, "col", 1, 4)) + (swap(sums, "col", 2, 4) + swap(sums, "col", 3, 4))
    theirs = swap(sums, "mp", 1, 2)
    margin, dy, dy_rest, grad_partial, rest_start = pl.pallas_call(
        functools.partial(score_kernel, seq_count),
        out_shape=(
            jax.ShapeDtypeStruct((1, tokens), F32),
            jax.ShapeDtypeStruct((main, features), BF16),
            jax.ShapeDtypeStruct((extra, features), BF16),
            jax.ShapeDtypeStruct((main, features), F32),
            jax.ShapeDtypeStruct((extra, features), F32),
        ),
        in_specs=[vmem] * 6,
        out_specs=(vmem,) * 5,
        compiler_params=pltpu.CompilerParams(vmem_limit_bytes=24 * 1024 * 1024),
        name="score",
    )(sums, theirs, scored, chosen, coeff, residual)
    loss_value = jnp.sum(jax.nn.softplus(-dpo_beta * margin)) / tokens

    rest_grad = rest.backward(dy_rest, rest_saved)
    for k, (start, width) in enumerate(cuts):
        near, far = times_rows(dy, down_proj, start, width)
        dhidden = reduce_to_ends(near, far)
        spread = spread_from_ends(pre_gradient(dhidden, *saved[k]), is_end)
        grad_partial = times_columns(grad_partial, *spread, weight, start)

    grads = jnp.concatenate([grad_partial, rest_grad + rest_start], axis=0)
    within = iota(square, 0) % (tokens // 2)
    block = within // eighth
    token = (
        iota(square, 0) // (tokens // 2) * (tokens // 2)
        + ((block % 2) * 2 + block // 2) * eighth
        + within % eighth
    )
    placed = lax.dot_general(
        (token == iota(square, 1)).astype(BF16),
        chosen,
        (((1,), (1,)), ((), ())),
        preferred_element_type=F32,
    ).astype(BF16)
    high = grads.astype(BF16)
    low = (grads - high.astype(F32)).astype(BF16)
    grads = jnp.dot(placed, high, preferred_element_type=F32) + jnp.dot(
        placed, low, preferred_element_type=F32
    )

    folded = grads.reshape(2, 2, 2 * eighth, features)
    keep = jnp.where(core_bit == 0, folded[:, 0], folded[:, 1])
    give = jnp.where(core_bit == 0, folded[:, 1], folded[:, 0])
    pair = keep + swap(give.astype(BF16), "row", 1, 4).astype(F32)
    folded = pair.reshape(2, 2, eighth, features)
    keep = jnp.where(chip_bit == 0, folded[:, 0], folded[:, 1])
    give = jnp.where(chip_bit == 0, folded[:, 1], folded[:, 0])
    give = give.astype(BF16)
    own_total = keep[0] + swap(give[0], "row", 2, 4).astype(F32)
    sent = lax.ppermute(keep[1].astype(BF16), "mp", [(0, 1)]).astype(F32)
    sent = sent + lax.ppermute(
        give[1], ("mp", "row"), [(i, 4 + (i ^ 2)) for i in range(4)]
    ).astype(F32)
    input_grad = jnp.where(is_policy, own_total, sent)
    return (loss_value, input_grad)


def solution(mesh):
    in_specs = (
        P("row", "col"),
        P(("mp", "row"), "col"),
        P(),
        P(),
        P("row"),
        P("mp", "col"),
        P("mp", "row", "col"),
        P("mp", "col", None, "row"),
        P("mp", "row", "col"),
    )
    out_specs = (P(), P(("mp", "row"), "col"))
    sizes = dict(mesh.shape)
    if not (sizes["mp"] == 2 and sizes["row"] == 4 and sizes["col"] == 4):
        return jax.shard_map(
            general, mesh=mesh, in_specs=in_specs, out_specs=out_specs, check_vma=False
        )

    return jax.shard_map(line_of_four, mesh=mesh, in_specs=in_specs, out_specs=out_specs, check_vma=False)
```
